32 devices in a mesh: gx: 2 (over y), gy: 4 (over z), gz: 4 (over x, core).
Axes of the slice: x: 2, y: 2, z: 4, core: 2. Of those that a mesh axis runs over, the one named last changes fastest.
Arguments:
- positions: float32 [4, 4, 4, 3, 32], P('gx', 'gy', 'gz'), may hold values from 0 to 5, as said below
- counts: int32 [4, 4, 4], P('gx', 'gy', 'gz'), may hold values from 1 to 32, as said below
- scalars: bfloat16 [4, 4, 4, 32, 128], P('gx', 'gy', 'gz'), may hold values from -6 to 6
- vectors: bfloat16 [4, 4, 4, 32, 3, 128], P('gx', 'gy', 'gz'), may hold values from -6 to 6
- radial_in: bfloat16 [2, 8, 64], replicated, may hold values from -2 to 2
- radial_bias: float32 [2, 64], replicated, may hold values from -3 to 3
- radial_out: bfloat16 [2, 64, 512], replicated, may hold values from -0.75 to 0.75
- atom_in: bfloat16 [2, 128, 128], replicated, may hold values from -0.5 to 0.5
- atom_bias: float32 [2, 128], replicated, may hold values from -3 to 3
- atom_out: bfloat16 [2, 128, 512], replicated, may hold values from -0.5 to 0.5
- readout_in: bfloat16 [128, 64], replicated, may hold values from -0.5 to 0.5
- readout_out: float32 [64], replicated, may hold values from -0.75 to 0.75
Outputs:
- scalars_out: bfloat16 [4, 4, 4, 32, 128], P('gx', 'gy', 'gz')
- vectors_out: bfloat16 [4, 4, 4, 32, 3, 128], P('gx', 'gy', 'gz')
- energy: float32 [1], replicated
The draws below stay inside these ranges and needn't reach their ends.
Inputs may be any that keep to these rules, and one draw needn't show every extreme that they name: `counts`: some cell of every draw holds 32 atoms and some other cell one atom. `positions`: the slots of a cell sit on distinct sites of a jittered lattice, so that any two slots, also of neighbouring cells, lie at least 0.5 apart.
All inputs are finite; a program needn't handle non-finite values.
Results may differ from the reference program's by a relative error of at most 0.0075.
Values may be sent and summed in bfloat16 or wider, within the bound.
A program may use at most 64 MiB of HBM per device.

```python
import math
import jax
import jax.numpy as jnp
from jax import lax

CHAN = 128
RADIAL = 64
BASIS = 8
FILTERS = 512
READOUT = 64
SLOTS = 32
LAYERS = 2
NX = 4
NY = 4
NZ = 4


def draw_counts(key, part):
    total = NX * NY * NZ
    key_extra, key_full, key_sparse = jax.random.split(key, 3)
    along = lax.broadcasted_iota(jnp.int32, (NX, NY, NZ), 0)
    level = along * (3 * SLOTS // 4) // NX
    extra = jax.random.randint(key_extra, (NX, NY, NZ), 1, SLOTS // 4 + 1)
    flat = jnp.minimum(level + extra, SLOTS).reshape(total)
    full_cell = jax.random.randint(key_full, (), 0, total)
    sparse_cell = (full_cell + 1 + jax.random.randint(key_sparse, (), 0, total - 1)) % total
    flat = flat.at[full_cell].set(SLOTS).at[sparse_cell].set(1)
    return flat.reshape(NX, NY, NZ).astype(jnp.int32)


def draw_positions(key, part):
    total = NX * NY * NZ
    key_order, key_shift = jax.random.split(key)

    def one_order(one_key):
        return jax.random.permutation(one_key, SLOTS)
    orders = jax.vmap(one_order)(jax.random.split(key_order, total))
    layers_z = SLOTS // 16
    site_x = (orders % 4).astype(jnp.float32)
    site_y = (orders // 4 % 4).astype(jnp.float32)
    site_z = (orders // 16).astype(jnp.float32)
    shift = jax.random.uniform(key_shift, (total, 3, SLOTS), jnp.float32, -0.3, 0.3)
    coords = jnp.stack([(site_x + 0.5 + shift[:, 0]) / 4.0, (site_y + 0.5 + shift[:, 1]) / 4.0, (site_z + 0.5 + shift[:, 2]) / layers_z], axis=1) * 5.0
    return coords.reshape(NX, NY, NZ, 3, SLOTS).astype(jnp.float32)


def level_of(key, shape, cuts, low, largest):
    def one(position, blocks):
        steps = jax.random.uniform(jax.random.fold_in(jax.random.fold_in(key, 6), position), (blocks,), jnp.float32, low / len(cuts), largest / len(cuts))
        return jnp.repeat(jnp.exp(steps), shape[position] // blocks).reshape((-1,) + (1,) * (len(shape) - position - 1))

    level = one(*cuts[0])
    for cut in cuts[1:]:
        level = level * one(*cut)
    return level


def normal_values(own_key, dims, scale, reach, pieces=(), kind=jnp.bfloat16):
    loudness = level_of(own_key, dims, pieces, -0.22, 0.18) if pieces else 1.0
    drawn = jax.random.normal(own_key, dims, jnp.float32) * scale * loudness
    return jnp.minimum(jnp.maximum(drawn, -reach), reach).astype(kind)


def setup_inputs(seed: int = 0) -> dict:
    keys = jax.random.split(jax.random.key(seed), 13)
    positions = draw_positions(jax.random.fold_in(keys[12], 71), 0)
    counts = draw_counts(jax.random.fold_in(keys[12], 71), 0)
    scalars = normal_values(keys[2], (NX, NY, NZ, SLOTS, CHAN), 1.0, 6.0, ((0, 2), (1, 4), (2, 4)))
    vectors = normal_values(keys[3], (NX, NY, NZ, SLOTS, 3, CHAN), 1.0, 6.0, ((0, 2), (1, 4), (2, 4)))
    radial_in = normal_values(keys[4], (LAYERS, BASIS, RADIAL), BASIS ** -0.5, 2.0)
    radial_bias = normal_values(keys[5], (LAYERS, RADIAL), 0.5, 3.0, (), jnp.float32)
    radial_out = normal_values(keys[6], (LAYERS, RADIAL, FILTERS), RADIAL ** -0.5, 0.75)
    atom_in = normal_values(keys[7], (LAYERS, CHAN, CHAN), CHAN ** -0.5, 0.5)
    atom_bias = normal_values(keys[8], (LAYERS, CHAN), 0.5, 3.0, (), jnp.float32)
    atom_out = normal_values(keys[9], (LAYERS, CHAN, FILTERS), CHAN ** -0.5, 0.5)
    readout_in = normal_values(keys[10], (CHAN, READOUT), CHAN ** -0.5, 0.5)
    readout_out = normal_values(keys[11], (READOUT,), READOUT ** -0.5, 0.75, (), jnp.float32)
    return {"positions": positions, "counts": counts, "scalars": scalars, "vectors": vectors, "radial_in": radial_in, "radial_bias": radial_bias, "radial_out": radial_out, "atom_in": atom_in, "atom_bias": atom_bias, "atom_out": atom_out, "readout_in": readout_in, "readout_out": readout_out}


cutoff = 5.0
message_scale = 0.5

def offsets_table():
    index = lax.broadcasted_iota(jnp.int32, (27, 3), 0)
    column = lax.broadcasted_iota(jnp.int32, (27, 3), 1)
    digit = jnp.where(column == 0, index // 9, jnp.where(column == 1, index // 3 % 3, index % 3))
    return (digit - 1).astype(jnp.float32)

def wrap_cells(field):
    widths = ((1, 1), (1, 1), (1, 1)) + ((0, 0),) * (field.ndim - 3)
    return jnp.pad(field, widths, mode='wrap')

def atom_gates(states, atom_in, atom_bias, atom_out):
    lead = states.shape[:-1]
    width = states.shape[-1]
    flat = states.reshape(-1, width)
    hidden = jax.nn.silu(jnp.dot(flat, atom_in, preferred_element_type=jnp.float32) + atom_bias).astype(jnp.bfloat16)
    gates = jnp.dot(hidden, atom_out, preferred_element_type=jnp.float32).astype(jnp.bfloat16)
    return gates.reshape(lead + (4, width))

def receiver_block(start, row_count, near_pos, near_live, own_pos, plain_side, gate_c, pair_g, radial_in, radial_bias, radial_out):
    slots = own_pos.shape[1]
    near_count = near_pos.shape[0]
    width = gate_c.shape[-1]
    mine = lax.dynamic_slice_in_dim(own_pos, start, row_count, 1).T
    displace = near_pos[None, :, :] - mine[:, None, :]
    row_index = start + lax.broadcasted_iota(jnp.int32, (row_count, near_count), 0)
    col_index = lax.broadcasted_iota(jnp.int32, (row_count, near_count), 1)
    itself = (col_index == row_index + 13 * slots).astype(jnp.float32)
    distance = jnp.sqrt(lax.optimization_barrier(jnp.sum(displace * displace, axis=-1)) + itself)
    unit = displace / distance[:, :, None]
    smooth = jnp.where(distance < cutoff, 0.5 * (jnp.cos(math.pi * distance / cutoff) + 1.0), 0.0)
    weight = smooth * near_live[None, :] * (1.0 - itself)
    basis_count = radial_in.shape[0]
    centers = lax.broadcasted_iota(jnp.float32, (basis_count,), 0) * (cutoff / (basis_count - 1))
    sharpness = 0.5 * ((basis_count - 1) / cutoff) ** 2
    basis = jnp.exp(-sharpness * (distance[:, :, None] - centers) ** 2).astype(jnp.bfloat16)
    hidden = jnp.dot(basis.reshape(-1, basis_count), radial_in, preferred_element_type=jnp.float32) + radial_bias
    hidden = jax.nn.silu(hidden).reshape(row_count, near_count, -1) * weight[:, :, None]
    edge = jnp.concatenate([hidden[:, :, None, :], hidden[:, :, None, :] * unit[:, :, :, None]], axis=2).astype(jnp.bfloat16)
    edge_plain = edge[:, :, 0, :].astype(jnp.float32)
    edge_turned = edge[:, :, 1:, :].astype(jnp.float32)
    scalar_part = jnp.einsum('rjh,jc->rhc', edge_plain, plain_side.astype(jnp.float32))
    along_part = jnp.einsum('rjkh,jf->rkhf', edge_turned, gate_c.astype(jnp.float32))
    project_part = jnp.einsum('rjkh,jkf->rhf', edge_turned, pair_g.astype(jnp.float32))
    filters = radial_out.astype(jnp.float32).reshape(-1, 4, width)
    term_a = scalar_part[:, :, :width]
    term_b = scalar_part[:, :, width:].reshape(row_count, -1, 3, width)
    scalar_delta = message_scale * (lax.optimization_barrier(jnp.sum(term_a * filters[None, :, 0, :], axis=1)) + lax.optimization_barrier(jnp.sum(project_part * filters[None, :, 3, :], axis=1)))
    vector_delta = message_scale * (lax.optimization_barrier(jnp.sum(term_b * filters[None, :, None, 1, :], axis=1)) + lax.optimization_barrier(jnp.sum(along_part * filters[None, None, :, 2, :], axis=2)))
    return (scalar_delta, vector_delta)

def cell_update(cell, geo_pad, feat_pad, scalar_state, vector_state, layer_params):
    radial_in, radial_bias, radial_out, atom_in, atom_bias, atom_out = layer_params
    grid_x, grid_y, grid_z, slots, width = scalar_state.shape
    at_x = cell // (grid_y * grid_z)
    at_y = cell // grid_z % grid_y
    at_z = cell % grid_z
    zero = jnp.zeros((), jnp.int32)
    geo_near = lax.dynamic_slice(geo_pad, (at_x, at_y, at_z, zero, zero), (3, 3, 3) + geo_pad.shape[3:]).reshape((27,) + geo_pad.shape[3:])
    feat_near = lax.dynamic_slice(feat_pad, (at_x, at_y, at_z, zero, zero, zero), (3, 3, 3) + feat_pad.shape[3:]).reshape((27 * slots,) + feat_pad.shape[4:])
    own_scalar = lax.dynamic_slice(scalar_state, (at_x, at_y, at_z, zero, zero), (1, 1, 1, slots, width)).reshape(slots, width)
    own_vector = lax.dynamic_slice(vector_state, (at_x, at_y, at_z, zero, zero, zero), (1, 1, 1, slots, 3, width)).reshape(slots, 3, width)
    near_pos = (geo_near[:, :3, :] + offsets_table()[:, :, None] * cutoff).transpose(0, 2, 1).reshape(27 * slots, 3)
    near_live = geo_near[:, 3, :].reshape(27 * slots)
    own_pos = geo_near[13, :3, :]
    own_live = geo_near[13, 3, :]
    gates = atom_gates(feat_near[:, 0, :], atom_in, atom_bias, atom_out)
    near_vectors = feat_near[:, 1:, :].astype(jnp.float32)
    pair_b = (gates[:, 1, None, :].astype(jnp.float32) * near_vectors).astype(jnp.bfloat16)
    pair_g = (gates[:, 3, None, :].astype(jnp.float32) * near_vectors).astype(jnp.bfloat16)
    plain_side = jnp.concatenate([gates[:, 0, :], pair_b.reshape(27 * slots, 3 * width)], axis=1)
    gate_c = gates[:, 2, :]
    row_count = slots // 8

    def one_block(block):
        start = block * row_count
        return receiver_block(start, row_count, near_pos, near_live, own_pos, plain_side, gate_c, pair_g, radial_in, radial_bias, radial_out)
    scalar_delta, vector_delta = lax.map(one_block, jnp.arange(8, dtype=jnp.int32))
    new_scalar = ((own_scalar.astype(jnp.float32) + scalar_delta.reshape(slots, width)) * own_live[:, None]).astype(jnp.bfloat16)
    new_vector = ((own_vector.astype(jnp.float32) + vector_delta.reshape(slots, 3, width)) * own_live[:, None, None]).astype(jnp.bfloat16)
    return (new_scalar, new_vector)

def reference(positions, counts, scalars, vectors, radial_in, radial_bias, radial_out, atom_in, atom_bias, atom_out, readout_in, readout_out):
    live = (lax.broadcasted_iota(jnp.int32, (NX, NY, NZ, SLOTS), 3) < counts[:, :, :, None]).astype(jnp.float32)
    geometry = jnp.concatenate([positions, live[:, :, :, None, :]], axis=3)
    geo_pad = wrap_cells(geometry)
    scalar_state, vector_state = (scalars, vectors)
    for layer in range(LAYERS):
        stacked = jnp.concatenate([scalar_state[:, :, :, :, None, :], vector_state], axis=4)
        feat_pad = wrap_cells(stacked)
        layer_params = (radial_in[layer], radial_bias[layer], radial_out[layer], atom_in[layer], atom_bias[layer], atom_out[layer])

        def one_cell(cell, feat_pad=feat_pad, scalar_state=scalar_state, vector_state=vector_state, layer_params=layer_params):
            return cell_update(cell, geo_pad, feat_pad, scalar_state, vector_state, layer_params)
        new_scalar, new_vector = lax.map(one_cell, jnp.arange(NX * NY * NZ, dtype=jnp.int32))
        scalar_state = new_scalar.reshape(NX, NY, NZ, SLOTS, CHAN)
        vector_state = new_vector.reshape(NX, NY, NZ, SLOTS, 3, CHAN)
    readout_hidden = jax.nn.silu(jnp.dot(scalar_state.reshape(-1, CHAN), readout_in, preferred_element_type=jnp.float32))
    atom_energy = lax.optimization_barrier(jnp.sum(readout_hidden * readout_out, axis=-1)) * live.reshape(-1)
    energy = jnp.sum(atom_energy).reshape(1)
    return (scalar_state, vector_state, energy)
```

```python
import functools
import math

import jax
import jax.numpy as jnp
from jax import lax
from jax.experimental import pallas as pl
from jax.experimental.pallas import tpu as pltpu
from jax.sharding import PartitionSpec as P

cutoff = 5.0
message_scale = 0.5
group = 8
chunk = 256


def extended(block, sides, width):
    for axis, dim in sides:
        count = lax.axis_size(axis)
        forward = [(i, i + 1) for i in range(count - 1)]
        forward.append((count - 1, 0))
        backward = [(target, source) for source, target in forward]
        low = lax.ppermute(
            lax.slice_in_dim(block, block.shape[dim] - width, None, axis=dim), axis, forward
        )
        high = lax.ppermute(lax.slice_in_dim(block, 0, width, axis=dim), axis, backward)
        block = jnp.concatenate([low, block, high], axis=dim)
    return block


def layer_kernel(
    grid_dims,
    max_chunks,
    counts,
    places,
    feats,
    radial_block,
    radial_bias,
    radial_out,
    atom_in,
    atom_bias,
    atom_out,
    out,
    near_place,
    near_state,
    place_rows,
    edges,
    plain_table,
    turned_table,
):
    deep, tall = grid_dims
    cell = pl.program_id(0)
    at_x = lax.div(cell, deep * tall)
    at_y = lax.rem(lax.div(cell, tall), deep)
    at_z = lax.rem(cell, tall)
    pad_y, pad_z = deep + 2, tall + 2
    slots = feats.shape[1]
    width = feats.shape[2] // 4
    hidden_width = radial_out.shape[0]
    basis_count = radial_block.shape[1] // group
    lane = lax.broadcasted_iota(jnp.int32, (slots, width), 1)

    def cell_index(dx, dy, dz):
        return ((at_x + dx) * pad_y + at_y + dy) * pad_z + at_z + dz

    home = cell_index(1, 1, 1)
    total = 0
    own_start = 0
    for dx in range(3):
        for dy in range(3):
            for dz in range(3):
                index = cell_index(dx, dy, dz)
                if (dx, dy, dz) == (1, 1, 1):
                    own_start = total
                shift = jnp.where(
                    lane == 0, float(dx - 1), jnp.where(lane == 1, float(dy - 1), float(dz - 1))
                )
                near_place[pl.ds(total, slots), :] = places[index] + shift * cutoff
                block = feats[index].astype(jnp.float32)
                for part in range(4):
                    near_state[part, pl.ds(total, slots), :] = block[
                        :, part * width : (part + 1) * width
                    ]
                total = total + counts[index]
    blank = jnp.zeros((chunk, width), jnp.float32)
    near_place[pl.ds(total, chunk), :] = blank
    for part in range(4):
        near_state[part, pl.ds(total, chunk), :] = blank
    chunks = lax.div(total + chunk - 1, chunk)

    @pl.loop(0, chunks)
    def _(step):
        rows = pl.ds(pl.multiple_of(step * chunk, chunk), chunk)
        place_rows[:, rows] = near_place[rows, :].T[:8, :]
        half = jnp.dot(
            near_state[0, rows, :].astype(jnp.bfloat16),
            atom_in[...],
            preferred_element_type=jnp.float32,
        ) + atom_bias[...]
        hidden = (half + half * jnp.tanh(half)).astype(jnp.bfloat16)
        gates = jnp.dot(hidden, atom_out[...], preferred_element_type=jnp.float32).astype(
            jnp.bfloat16
        )
        plain_table[rows, :width] = gates[:, :width]
        gate_b = gates[:, width : 2 * width].astype(jnp.float32)
        gate_c = gates[:, 2 * width : 3 * width]
        gate_g = gates[:, 3 * width :].astype(jnp.float32)
        for part in range(3):
            vector = near_state[part + 1, rows, :]
            plain_table[rows, (part + 1) * width : (part + 2) * width] = (gate_b * vector).astype(
                jnp.bfloat16
            )
            turned_table[part, rows, :width] = gate_c
            turned_table[part, rows, width:] = (gate_g * vector).astype(jnp.bfloat16)

    own_count = counts[home]
    out[0] = jnp.zeros(out.shape[1:], out.dtype)
    sharpness = 0.5 * ((basis_count - 1) / cutoff) ** 2

    @pl.loop(0, lax.div(own_count + group - 1, group))
    def _(turn):
        first = pl.multiple_of(turn * group, group)
        mine = places[home, pl.ds(first, group), :]

        @pl.loop(0, chunks)
        def _(step):
            columns = pl.ds(pl.multiple_of(step * chunk, chunk), chunk)
            col = step * chunk + lax.broadcasted_iota(jnp.int32, (group, chunk), 1)
            row = first + lax.broadcasted_iota(jnp.int32, (group, chunk), 0)
            unused = jnp.logical_or(col == own_start + row, col >= total)
            offset = [place_rows[k : k + 1, columns] - mine[:, k : k + 1] for k in range(3)]
            square = offset[0] * offset[0] + offset[1] * offset[1] + offset[2] * offset[2]
            distance = jnp.sqrt(square + jnp.where(unused, 1.0, 0.0))
            inverse = 1.0 / distance
            smooth = 0.5 * (jnp.cos(math.pi / cutoff * distance) + 1.0)
            weight = jnp.where(
                jnp.logical_and(distance < cutoff, jnp.logical_not(unused)), smooth, 0.0
            )
            centers = lax.broadcasted_iota(jnp.int32, (1, basis_count, chunk), 1).astype(
                jnp.float32
            ) * (cutoff / (basis_count - 1))
            gap = distance[:, None, :] - centers
            basis = jnp.exp(-sharpness * gap * gap).reshape(group * basis_count, chunk)
            half = jnp.dot(
                radial_block[...], basis.astype(jnp.bfloat16), preferred_element_type=jnp.float32
            ).reshape(group, hidden_width, chunk) + radial_bias[...][None]
            active = (half + half * jnp.tanh(half)) * weight[:, None, :]
            edges[0, :, columns] = active.reshape(group * hidden_width, chunk).astype(jnp.bfloat16)
            for k in range(3):
                unit = (offset[k] * inverse)[:, None, :]
                edges[k + 1, :, columns] = (
                    (active * unit).reshape(group * hidden_width, chunk).astype(jnp.bfloat16)
                )

        for used in range(1, max_chunks + 1):

            @pl.when(chunks == used)
            def _(used=used):
                span = used * chunk

                def contracted(left, right, filters):
                    product = jnp.dot(left, right, preferred_element_type=jnp.float32)
                    product = product.reshape(group, hidden_width, 2 * width)
                    return (
                        jnp.sum(product[:, :, :width] * filters[0], axis=1),
                        jnp.sum(product[:, :, width:] * filters[1], axis=1),
                    )

                bank = [
                    radial_out[:, part * width : (part + 1) * width].astype(jnp.float32)[None]
                    for part in range(4)
                ]
                flat = edges[0, :, :span]
                scalar, vector0 = contracted(flat, plain_table[:span, : 2 * width], (bank[0], bank[1]))
                vector1, vector2 = contracted(flat, plain_table[:span, 2 * width :], (bank[1], bank[1]))
                vectors = [vector0, vector1, vector2]
                for k in range(3):
                    along, project = contracted(
                        edges[k + 1, :, :span], turned_table[k, :span, :], (bank[2], bank[3])
                    )
                    vectors[k] = vectors[k] + along
                    scalar = scalar + project
                receivers = first + lax.broadcasted_iota(jnp.int32, (group, width), 0)
                alive = receivers < own_count
                for part, change in enumerate([scalar] + vectors):
                    before = near_state[part, pl.ds(own_start + first, group), :]
                    after = jnp.where(alive, before + message_scale * change, 0.0)
                    out[0, pl.ds(first, group), part * width : (part + 1) * width] = after


def layer_update(cells_shape, counts, places, feats, params):
    cells_wide, cells_deep, cells_tall = cells_shape
    radial_in, radial_bias, radial_out, atom_in, atom_bias, atom_out = params
    total_cells = cells_wide * cells_deep * cells_tall
    slots = feats.shape[1]
    width = feats.shape[2] // 4
    hidden_width = radial_in.shape[1]
    max_chunks = -(-27 * slots // chunk)
    radial_block = jnp.kron(jnp.eye(group, dtype=jnp.float32), 0.5 * radial_in.astype(jnp.float32).T)
    span = max_chunks * chunk
    store = 27 * slots + chunk + slots
    store = -(-store // 8) * 8
    vmem = pl.BlockSpec(memory_space=pltpu.VMEM)
    return pl.pallas_call(
        functools.partial(layer_kernel, (cells_deep, cells_tall), max_chunks),
        grid=(total_cells,),
        out_shape=jax.ShapeDtypeStruct((total_cells, slots, 4 * width), jnp.float32),
        in_specs=[pl.BlockSpec(memory_space=pltpu.SMEM)] + [vmem] * 8,
        out_specs=pl.BlockSpec((1, slots, 4 * width), lambda i: (i, 0, 0)),
        scratch_shapes=[
            pltpu.VMEM((store, width), jnp.float32),
            pltpu.VMEM((4, store, width), jnp.float32),
            pltpu.VMEM((8, span), jnp.float32),
            pltpu.VMEM((4, group * hidden_width, span), jnp.bfloat16),
            pltpu.VMEM((span, 4 * width), jnp.bfloat16),
            pltpu.VMEM((3, span, 2 * width), jnp.bfloat16),
        ],
        compiler_params=pltpu.CompilerParams(vmem_limit_bytes=56 << 20),
        name="message_layer",
    )(
        counts,
        places,
        feats,
        radial_block.astype(jnp.bfloat16),
        jnp.broadcast_to(0.5 * radial_bias[:, None], (hidden_width, chunk)),
        radial_out,
        (0.5 * atom_in.astype(jnp.float32)).astype(jnp.bfloat16),
        0.5 * atom_bias[None, :],
        atom_out,
    )


def summed(value, axes):
    for axis in axes:
        count = lax.axis_size(axis)
        if count & (count - 1):
            value = lax.psum(value, axis)
            continue
        step = 1
        while step < count:
            value = value + lax.ppermute(value, axis, [(i, i ^ step) for i in range(count)])
            step *= 2
    return value


def on_device(
    positions,
    counts,
    scalars,
    vectors,
    radial_in,
    radial_bias,
    radial_out,
    atom_in,
    atom_bias,
    atom_out,
    readout_in,
    readout_out,
):
    cells_wide, cells_deep, cells_tall, slots, width = scalars.shape
    cells_shape = (cells_wide, cells_deep, cells_tall)
    sides = (("gy", 1), ("gx", 0), ("gz", 2))
    live = (
        lax.broadcasted_iota(jnp.int32, cells_shape + (slots,), 3) < counts[:, :, :, None]
    ).astype(jnp.float32)
    level = jnp.broadcast_to(counts.astype(jnp.float32)[..., None, None], cells_shape + (1, slots))
    geometry = extended(jnp.concatenate([positions, level], axis=3), sides, 1)
    near_counts = geometry[:, :, :, 3, 0].astype(jnp.int32).reshape(-1)
    places = geometry.reshape((-1,) + geometry.shape[3:]).transpose(0, 2, 1)
    places = jnp.pad(places, ((0, 0), (0, 0), (0, width - places.shape[2])))
    state = jnp.concatenate(
        [scalars, vectors.reshape(cells_shape + (slots, 3 * width))], axis=-1
    )
    for layer in range(radial_in.shape[0]):
        params = (
            radial_in[layer],
            radial_bias[layer],
            radial_out[layer],
            atom_in[layer],
            atom_bias[layer],
            atom_out[layer],
        )
        feats = extended(state, sides, 1)
        state = layer_update(
            cells_shape, near_counts, places, feats.reshape(-1, slots, 4 * width), params
        )
        state = state.astype(jnp.bfloat16).reshape(cells_shape + (slots, 4 * width))
    scalar_state = state[..., :width]
    vector_state = state[..., width:].reshape(cells_shape + (slots, 3, width))
    readout_hidden = jax.nn.silu(
        jnp.dot(scalar_state.reshape(-1, width), readout_in, preferred_element_type=jnp.float32)
    )
    atom_energy = jnp.sum(readout_hidden * readout_out, axis=-1) * live.reshape(-1)
    energy = summed(jnp.sum(atom_energy).reshape(1), ("gx", "gy", "gz"))
    return (scalar_state, vector_state, energy)


def solution(mesh):
    block = P("gx", "gy", "gz")
    in_specs = (block,) * 4 + (P(),) * 8
    out_specs = (block, block, P())
    return jax.shard_map(
        on_device, mesh=mesh, in_specs=in_specs, out_specs=out_specs, check_vma=False
    )
```

```python
import functools
import math

import jax
import jax.numpy as jnp
from jax import lax
from jax.experimental import pallas as pl
from jax.experimental.pallas import tpu as pltpu
from jax.sharding import PartitionSpec as P

cutoff = 5.0
message_scale = 0.5
group = 8
chunk = 256


MESH = pl.DeviceIdType.MESH
pieces = 4
sides = (("gy", 1), ("gx", 0), ("gz", 2))


def ring(axis):
    me = lax.axis_index(axis)
    count = lax.axis_size(axis)
    return lax.rem(me + 1, count), lax.rem(me + count - 1, count)


def halo_kernel(array_count, *refs):
    blocks = refs[:array_count]
    pads = refs[array_count : 2 * array_count]
    local_sem, send_sem, recv_sem = refs[2 * array_count :]
    dims = blocks[0].shape[:3]
    around = {axis: ring(axis) for axis, _ in sides}
    barrier = pltpu.get_barrier_semaphore()
    for axis, _ in sides:
        for side in around[axis]:
            pl.semaphore_signal(barrier, inc=1, device_id={axis: side}, device_id_type=MESH)
    units = []
    for block, pad in zip(blocks, pads):
        lanes = block.shape[-1]
        cuts = pieces if lanes % (128 * pieces) == 0 else 1
        for cut in range(cuts):
            units.append((block, pad, pl.ds(cut * (lanes // cuts), lanes // cuts)))
    units = units[::-1] if array_count > 1 else units
    center = tuple(pl.ds(1, extent) for extent in dims)
    own = []
    for place, (block, pad) in enumerate(zip(blocks, pads)):
        own.append(pltpu.make_async_copy(block, pad.at[center], local_sem.at[place]))
        own[-1].start()
    pl.semaphore_wait(barrier, 2 * len(sides))
    sent = {}

    def send(stage, number):
        block, pad, lanes = units[number]
        axis, dim = sides[stage]
        done = [d for _, d in sides[:stage]]
        extent = dims[dim]
        for way, (source, target) in enumerate(((extent, 0), (1, extent + 1))):
            region = [
                pl.ds(0, dims[d] + 2) if d in done else pl.ds(1, dims[d]) for d in range(3)
            ]
            region[dim] = pl.ds(target, 1)
            to = pad.at[tuple(region) + (slice(None), lanes)]
            if stage == 0:
                region = [pl.ds(0, dims[d]) for d in range(3)]
                region[dim] = pl.ds(source - 1, 1)
                come = block.at[tuple(region) + (slice(None), lanes)]
            else:
                region[dim] = pl.ds(source, 1)
                come = pad.at[tuple(region) + (slice(None), lanes)]
            copy = pltpu.make_async_remote_copy(
                src_ref=come,
                dst_ref=to,
                send_sem=send_sem.at[stage, way, number],
                recv_sem=recv_sem.at[stage, way, number],
                device_id={axis: around[axis][way]},
                device_id_type=MESH,
            )
            copy.start()
            sent[stage, way, number] = copy

    for number in range(len(units)):
        send(0, number)
    for copy in own:
        copy.wait()
    for stage in range(1, len(sides) + 1):
        for number in range(len(units)):
            for way in range(2):
                sent[stage - 1, way, number].wait_recv()
            if stage < len(sides):
                send(stage, number)
    for copy in sent.values():
        copy.wait_send()


def extended(blocks, identity):
    dims = blocks[0].shape[:3]
    vmem = pl.BlockSpec(memory_space=pltpu.VMEM)
    count = sum(pieces if block.shape[-1] % (128 * pieces) == 0 else 1 for block in blocks)
    return pl.pallas_call(
        functools.partial(halo_kernel, len(blocks)),
        out_shape=[
            jax.ShapeDtypeStruct(tuple(d + 2 for d in dims) + block.shape[3:], block.dtype)
            for block in blocks
        ],
        in_specs=[vmem] * len(blocks),
        out_specs=[vmem] * len(blocks),
        scratch_shapes=[
            pltpu.SemaphoreType.DMA((len(blocks),)),
            pltpu.SemaphoreType.DMA((len(sides), 2, count)),
            pltpu.SemaphoreType.DMA((len(sides), 2, count)),
        ],
        compiler_params=pltpu.CompilerParams(collective_id=identity, has_side_effects=True),
        name="halo",
    )(*blocks)


def total_kernel(axes, part, out, held, local_sem, send_sem, recv_sem):
    barrier = pltpu.get_barrier_semaphore()
    sizes = [lax.axis_size(axis) for axis in axes]
    places = [lax.axis_index(axis) for axis in axes]
    greeted = 0
    for axis, size, me in zip(axes, sizes, places):
        for step in range(1, size):
            pl.semaphore_signal(
                barrier, inc=1, device_id={axis: lax.rem(me + step, size)}, device_id_type=MESH
            )
            greeted += 1
    own = pltpu.make_async_copy(part, held.at[places[2], places[1], places[0]], local_sem)
    own.start()
    pl.semaphore_wait(barrier, greeted)
    own.wait()
    for stage, (axis, size, me) in enumerate(zip(axes, sizes, places)):
        if stage == 0:
            view = held.at[places[2], places[1], places[0]]
        elif stage == 1:
            view = held.at[places[2], places[1]]
        else:
            view = held.at[places[2]]
        copies = []
        for step in range(1, size):
            copy = pltpu.make_async_remote_copy(
                src_ref=view,
                dst_ref=view,
                send_sem=send_sem.at[stage, step],
                recv_sem=recv_sem.at[stage, step],
                device_id={axis: lax.rem(me + step, size)},
                device_id_type=MESH,
            )
            copy.start()
            copies.append(copy)
        for copy in copies:
            copy.wait()
    out[...] = jnp.sum(held[...], axis=(0, 1, 2))


def summed(part, axes, identity):
    sizes = [lax.axis_size(axis) for axis in axes]
    vmem = pl.BlockSpec(memory_space=pltpu.VMEM)
    return pl.pallas_call(
        functools.partial(total_kernel, axes),
        out_shape=jax.ShapeDtypeStruct(part.shape, part.dtype),
        in_specs=[vmem],
        out_specs=vmem,
        scratch_shapes=[
            pltpu.VMEM((sizes[2], sizes[1], sizes[0]) + part.shape, part.dtype),
            pltpu.SemaphoreType.DMA,
            pltpu.SemaphoreType.DMA((3, max(sizes))),
            pltpu.SemaphoreType.DMA((3, max(sizes))),
        ],
        compiler_params=pltpu.CompilerParams(collective_id=identity, has_side_effects=True),
        name="total",
    )(part)


def layer_kernel(
    grid_dims,
    max_chunks,
    layer,
    counts,
    ground,
    feats,
    radial_in_all,
    radial_bias_all,
    radial_out_all,
    atom_in_all,
    atom_bias_all,
    atom_out_all,
    readout_in,
    readout_out,
    out,
    part_out,
    places,
    radial_block,
    radial_bias,
    fresh,
    near_place,
    near_state,
    place_rows,
    edges,
    plain_table,
    turned_table,
):
    deep, tall = grid_dims
    cell = pl.program_id(0)
    at_x = lax.div(cell, deep * tall)
    at_y = lax.rem(lax.div(cell, tall), deep)
    at_z = lax.rem(cell, tall)
    pad_y, pad_z = deep + 2, tall + 2
    slots = feats.shape[1]
    width = feats.shape[2] // 4
    radial_out = radial_out_all.at[layer]
    atom_out = atom_out_all.at[layer]
    basis_count, hidden_width = radial_in_all.shape[1:]

    @pl.when(cell == 0)
    def _():
        part_out[...] = jnp.zeros(part_out.shape, part_out.dtype)
        small = 0.5 * radial_in_all[layer].astype(jnp.float32)
        tall_form = jnp.concatenate([small] * group, axis=0)
        wide_form = jnp.concatenate([tall_form] * (128 // hidden_width), axis=1).T[:hidden_width]
        box = (group, hidden_width, group * basis_count)
        spread = jnp.broadcast_to(wide_form[None], box)
        owner = lax.div(lax.broadcasted_iota(jnp.int32, box, 2), basis_count)
        spread = jnp.where(owner == lax.broadcasted_iota(jnp.int32, box, 0), spread, 0.0)
        radial_block[...] = spread.reshape(radial_block.shape).astype(jnp.bfloat16)
        bias = 0.5 * radial_bias_all[layer : layer + 1, :]
        bias = jnp.concatenate([bias] * (128 // hidden_width), axis=1)
        radial_bias[...] = jnp.broadcast_to(bias, (chunk, 128)).T[:hidden_width]

        @pl.loop(0, ground.shape[0])
        def _(index):
            places[index, :, :8] = ground[index].T[:slots, :]

    lane = lax.broadcasted_iota(jnp.int32, (slots, width), 1)

    def cell_index(dx, dy, dz):
        return ((at_x + dx) * pad_y + at_y + dy) * pad_z + at_z + dz

    home = cell_index(1, 1, 1)
    total = 0
    own_start = 0
    for dx in range(3):
        for dy in range(3):
            for dz in range(3):
                index = cell_index(dx, dy, dz)
                if (dx, dy, dz) == (1, 1, 1):
                    own_start = total
                shift = jnp.where(
                    lane == 0, float(dx - 1), jnp.where(lane == 1, float(dy - 1), float(dz - 1))
                )
                near_place[pl.ds(total, slots), :] = places[index] + shift * cutoff
                block = feats[index].astype(jnp.float32)
                for part in range(4):
                    near_state[part, pl.ds(total, slots), :] = block[
                        :, part * width : (part + 1) * width
                    ]
                total = total + counts[index]
    blank = jnp.zeros((chunk, width), jnp.float32)
    near_place[pl.ds(total, chunk), :] = blank
    for part in range(4):
        near_state[part, pl.ds(total, chunk), :] = blank
    chunks = lax.div(total + chunk - 1, chunk)

    @pl.loop(0, chunks)
    def _(step):
        rows = pl.ds(pl.multiple_of(step * chunk, chunk), chunk)
        place_rows[:, rows] = near_place[rows, :].T[:8, :]
        half = jnp.dot(
            near_state[0, rows, :].astype(jnp.bfloat16),
            (0.5 * atom_in_all[layer].astype(jnp.float32)).astype(jnp.bfloat16),
            preferred_element_type=jnp.float32,
        ) + 0.5 * atom_bias_all[layer : layer + 1, :]
        hidden = (half + half * jnp.tanh(half)).astype(jnp.bfloat16)
        gates = jnp.dot(hidden, atom_out[...], preferred_element_type=jnp.float32).astype(
            jnp.bfloat16
        )
        plain_table[rows, :width] = gates[:, :width]
        gate_b = gates[:, width : 2 * width].astype(jnp.float32)
        gate_c = gates[:, 2 * width : 3 * width]
        gate_g = gates[:, 3 * width :].astype(jnp.float32)
        for part in range(3):
            vector = near_state[part + 1, rows, :]
            plain_table[rows, (part + 1) * width : (part + 2) * width] = (gate_b * vector).astype(
                jnp.bfloat16
            )
            turned_table[part, rows, :width] = gate_c
            turned_table[part, rows, width:] = (gate_g * vector).astype(jnp.bfloat16)

    own_count = counts[home]
    fresh[...] = jnp.zeros(fresh.shape, fresh.dtype)
    sharpness = 0.5 * ((basis_count - 1) / cutoff) ** 2

    @pl.loop(0, lax.div(own_count + group - 1, group))
    def _(turn):
        first = pl.multiple_of(turn * group, group)
        mine = places[home, pl.ds(first, group), :]

        @pl.loop(0, chunks)
        def _(step):
            columns = pl.ds(pl.multiple_of(step * chunk, chunk), chunk)
            col = step * chunk + lax.broadcasted_iota(jnp.int32, (group, chunk), 1)
            row = first + lax.broadcasted_iota(jnp.int32, (group, chunk), 0)
            unused = jnp.logical_or(col == own_start + row, col >= total)
            offset = [place_rows[k : k + 1, columns] - mine[:, k : k + 1] for k in range(3)]
            square = offset[0] * offset[0] + offset[1] * offset[1] + offset[2] * offset[2]
            distance = jnp.sqrt(square + jnp.where(unused, 1.0, 0.0))
            inverse = 1.0 / distance
            smooth = 0.5 * (jnp.cos(math.pi / cutoff * distance) + 1.0)
            weight = jnp.where(
                jnp.logical_and(distance < cutoff, jnp.logical_not(unused)), smooth, 0.0
            )
            centers = lax.broadcasted_iota(jnp.int32, (1, basis_count, chunk), 1).astype(
                jnp.float32
            ) * (cutoff / (basis_count - 1))
            gap = distance[:, None, :] - centers
            basis = jnp.exp(-sharpness * gap * gap).reshape(group * basis_count, chunk)
            half = jnp.dot(
                radial_block[...], basis.astype(jnp.bfloat16), preferred_element_type=jnp.float32
            ).reshape(group, hidden_width, chunk) + radial_bias[...][None]
            active = (half + half * jnp.tanh(half)) * weight[:, None, :]
            edges[0, :, columns] = active.reshape(group * hidden_width, chunk).astype(jnp.bfloat16)
            for k in range(3):
                unit = (offset[k] * inverse)[:, None, :]
                edges[k + 1, :, columns] = (
                    (active * unit).reshape(group * hidden_width, chunk).astype(jnp.bfloat16)
                )

        for used in range(1, max_chunks + 1):

            @pl.when(chunks == used)
            def _(used=used):
                span = used * chunk

                def contracted(left, right, filters):
                    product = jnp.dot(left, right, preferred_element_type=jnp.float32)
                    product = product.reshape(group, hidden_width, 2 * width)
                    return (
                        jnp.sum(product[:, :, :width] * filters[0], axis=1),
                        jnp.sum(product[:, :, width:] * filters[1], axis=1),
                    )

                bank = [
                    radial_out[:, part * width : (part + 1) * width].astype(jnp.float32)[None]
                    for part in range(4)
                ]
                flat = edges[0, :, :span]
                scalar, vector0 = contracted(flat, plain_table[:span, : 2 * width], (bank[0], bank[1]))
                vector1, vector2 = contracted(flat, plain_table[:span, 2 * width :], (bank[1], bank[1]))
                vectors = [vector0, vector1, vector2]
                for k in range(3):
                    along, project = contracted(
                        edges[k + 1, :, :span], turned_table[k, :span, :], (bank[2], bank[3])
                    )
                    vectors[k] = vectors[k] + along
                    scalar = scalar + project
                receivers = first + lax.broadcasted_iota(jnp.int32, (group, width), 0)
                alive = receivers < own_count
                for part, change in enumerate([scalar] + vectors):
                    before = near_state[part, pl.ds(own_start + first, group), :]
                    after = jnp.where(alive, before + message_scale * change, 0.0)
                    fresh[pl.ds(first, group), part * width : (part + 1) * width] = after

    rounded = fresh[...].astype(jnp.bfloat16)
    out[0] = rounded
    if layer == radial_in_all.shape[0] - 1:
        read = jnp.dot(rounded[:, :width], readout_in[...], preferred_element_type=jnp.float32)
        read = read / (1.0 + jnp.exp(-read)) * readout_out[...]
        alive = lax.broadcasted_iota(jnp.int32, read.shape, 0) < own_count
        amount = jnp.sum(jnp.where(alive, read, 0.0), axis=(0, 1), keepdims=True)
        part_out[...] += jnp.broadcast_to(amount, part_out.shape)


def layer_update(layer, cells_shape, counts, ground, feats, params):
    cells_wide, cells_deep, cells_tall = cells_shape
    total_cells = cells_wide * cells_deep * cells_tall
    slots = feats.shape[1]
    width = feats.shape[2] // 4
    basis_count, hidden_width = params[0].shape[1:]
    max_chunks = -(-27 * slots // chunk)
    span = max_chunks * chunk
    store = 27 * slots + chunk + slots
    store = -(-store // 8) * 8
    vmem = pl.BlockSpec(memory_space=pltpu.VMEM)
    return pl.pallas_call(
        functools.partial(layer_kernel, (cells_deep, cells_tall), max_chunks, layer),
        grid=(total_cells,),
        out_shape=(
            jax.ShapeDtypeStruct((total_cells, slots, 4 * width), jnp.bfloat16),
            jax.ShapeDtypeStruct((8, 128), jnp.float32),
        ),
        in_specs=[pl.BlockSpec(memory_space=pltpu.SMEM)] + [vmem] * (2 + len(params)),
        out_specs=(
            pl.BlockSpec((1, slots, 4 * width), lambda i: (i, 0, 0)),
            pl.BlockSpec((8, 128), lambda i: (0, 0)),
        ),
        scratch_shapes=[
            pltpu.VMEM((ground.shape[0], slots, width), jnp.float32),
            pltpu.VMEM((group * hidden_width, group * basis_count), jnp.bfloat16),
            pltpu.VMEM((hidden_width, chunk), jnp.float32),
            pltpu.VMEM((slots, 4 * width), jnp.float32),
            pltpu.VMEM((store, width), jnp.float32),
            pltpu.VMEM((4, store, width), jnp.float32),
            pltpu.VMEM((8, span), jnp.float32),
            pltpu.VMEM((4, group * hidden_width, span), jnp.bfloat16),
            pltpu.VMEM((span, 4 * width), jnp.bfloat16),
            pltpu.VMEM((3, span, 2 * width), jnp.bfloat16),
        ],
        compiler_params=pltpu.CompilerParams(vmem_limit_bytes=56 << 20),
        name="message_layer",
    )(counts, ground, feats, *params)


def on_device(
    positions,
    counts,
    scalars,
    vectors,
    radial_in,
    radial_bias,
    radial_out,
    atom_in,
    atom_bias,
    atom_out,
    readout_in,
    readout_out,
):
    cells_wide, cells_deep, cells_tall, slots, width = scalars.shape
    cells_shape = (cells_wide, cells_deep, cells_tall)
    level = jnp.broadcast_to(counts.astype(jnp.float32)[..., None, None], cells_shape + (1, slots))
    geometry = jnp.concatenate([positions, level], axis=3)
    geometry = jnp.pad(geometry, ((0, 0),) * 3 + ((0, 8 - geometry.shape[3]), (0, 128 - slots)))
    state = jnp.concatenate(
        [scalars, vectors.reshape(cells_shape + (slots, 3 * width))], axis=-1
    )
    params = (
        radial_in,
        radial_bias,
        radial_out,
        atom_in,
        atom_bias,
        atom_out,
        readout_in,
        readout_out[None, :],
    )
    for layer in range(radial_in.shape[0]):
        if layer == 0:
            feats, ground = extended([state, geometry], 0)
            ground = ground.reshape((-1,) + ground.shape[3:])
            near_counts = ground[:, 3, 0].astype(jnp.int32)
        else:
            (feats,) = extended([state], layer)
        state, part = layer_update(
            layer, cells_shape, near_counts, ground, feats.reshape(-1, slots, 4 * width), params
        )
        state = state.reshape(cells_shape + (slots, 4 * width))
    scalar_state = state[..., :width]
    vector_state = state[..., width:].reshape(cells_shape + (slots, 3, width))
    energy = summed(part, ("gz", "gx", "gy"), radial_in.shape[0])[0, :1]
    return (scalar_state, vector_state, energy)


def solution(mesh):
    block = P("gx", "gy", "gz")
    in_specs = (block,) * 4 + (P(),) * 8
    out_specs = (block, block, P())
    return jax.shard_map(
        on_device, mesh=mesh, in_specs=in_specs, out_specs=out_specs, check_vma=False
    )
```

```python
import functools
import math

import jax
import jax.numpy as jnp
from jax import lax
from jax.experimental import pallas as pl
from jax.experimental.pallas import tpu as pltpu
from jax.sharding import PartitionSpec as P

cutoff = 5.0
message_scale = 0.5
group = 8
chunk = 256


MESH = pl.DeviceIdType.MESH
pieces = 4
sides = (("gy", 1), ("gx", 0), ("gz", 2))


def ring(axis):
    me = lax.axis_index(axis)
    count = lax.axis_size(axis)
    return lax.rem(me + 1, count), lax.rem(me + count - 1, count)


def prepare(ground, radial_in, radial_bias, places, counts, radial_block, bias_wide):
    wide, deep, tall = ground.shape[:3]
    slots = places.shape[1]
    layers, basis_count, hidden_width = radial_in.shape
    for x in range(wide):
        for y in range(deep):
            for z in range(tall):
                index = (x * deep + y) * tall + z
                tile = ground[x, y, z]
                places[index, :, :8] = tile.T[:slots, :]
                counts[index : index + 1, :] = tile[3:4, :].astype(jnp.int32)
    box = (group, hidden_width, group * basis_count)
    owner = lax.div(lax.broadcasted_iota(jnp.int32, box, 2), basis_count)
    match = owner == lax.broadcasted_iota(jnp.int32, box, 0)
    for layer in range(layers):
        small = 0.5 * radial_in[layer].astype(jnp.float32)
        tall_form = jnp.concatenate([small] * group, axis=0)
        wide_form = jnp.concatenate([tall_form] * (128 // hidden_width), axis=1).T[:hidden_width]
        spread = jnp.where(match, jnp.broadcast_to(wide_form[None], box), 0.0)
        radial_block[layer] = spread.reshape(radial_block.shape[1:]).astype(jnp.bfloat16)
        bias = 0.5 * radial_bias[layer : layer + 1, :]
        bias = jnp.concatenate([bias] * (128 // hidden_width), axis=1)
        bias_wide[layer] = jnp.broadcast_to(bias, (chunk, 128)).T[:hidden_width]


def halo_kernel(first, *refs):
    if first:
        state, geometry, radial_in, radial_bias, feats, *made = refs[:9]
        ground, local_sem, send_sem, recv_sem = refs[9:]
        blocks, pads = [state, geometry], [feats, ground]
    else:
        state, feats, local_sem, send_sem, recv_sem = refs
        blocks, pads = [state], [feats]
    dims = blocks[0].shape[:3]
    around = {axis: ring(axis) for axis, _ in sides}
    barrier = pltpu.get_barrier_semaphore()
    for axis, _ in sides:
        for side in around[axis]:
            pl.semaphore_signal(barrier, inc=1, device_id={axis: side}, device_id_type=MESH)
    units = []
    for block, pad in zip(blocks, pads):
        lanes = block.shape[-1]
        cuts = pieces if lanes % (128 * pieces) == 0 else 1
        for cut in range(cuts):
            units.append((block, pad, pl.ds(cut * (lanes // cuts), lanes // cuts)))
    units = units[::-1]
    center = tuple(pl.ds(1, extent) for extent in dims)
    own = []
    for place, (block, pad) in enumerate(zip(blocks, pads)):
        own.append(pltpu.make_async_copy(block, pad.at[center], local_sem.at[place]))
        own[-1].start()
    pl.semaphore_wait(barrier, 2 * len(sides))
    sent = {}

    def send(stage, number):
        block, pad, lanes = units[number]
        axis, dim = sides[stage]
        done = [d for _, d in sides[:stage]]
        extent = dims[dim]
        for way, (source, target) in enumerate(((extent, 0), (1, extent + 1))):
            region = [
                pl.ds(0, dims[d] + 2) if d in done else pl.ds(1, dims[d]) for d in range(3)
            ]
            region[dim] = pl.ds(target, 1)
            to = pad.at[tuple(region) + (slice(None), lanes)]
            if stage == 0:
                region = [pl.ds(0, dims[d]) for d in range(3)]
                region[dim] = pl.ds(source - 1, 1)
                come = block.at[tuple(region) + (slice(None), lanes)]
            else:
                region[dim] = pl.ds(source, 1)
                come = pad.at[tuple(region) + (slice(None), lanes)]
            copy = pltpu.make_async_remote_copy(
                src_ref=come,
                dst_ref=to,
                send_sem=send_sem.at[stage, way, number],
                recv_sem=recv_sem.at[stage, way, number],
                device_id={axis: around[axis][way]},
                device_id_type=MESH,
            )
            copy.start()
            sent[stage, way, number] = copy

    for number in range(len(units)):
        send(0, number)
    for copy in own:
        copy.wait()
    for stage in range(1, len(sides) + 1):
        for number in range(len(units)):
            for way in range(2):
                sent[stage - 1, way, number].wait_recv()
            if stage < len(sides):
                send(stage, number)
            elif number == 0 and first:
                prepare(ground, radial_in, radial_bias, *made)
    for copy in sent.values():
        copy.wait_send()


def extended(state, identity, extra=()):
    dims = state.shape[:3]
    slots = state.shape[3]
    vmem = pl.BlockSpec(memory_space=pltpu.VMEM)
    outer = tuple(d + 2 for d in dims)
    cells = math.prod(outer)
    shapes = [jax.ShapeDtypeStruct(outer + state.shape[3:], state.dtype)]
    scratch = []
    units = pieces if state.shape[-1] % (128 * pieces) == 0 else 1
    if extra:
        layers, basis_count, hidden_width = extra[1].shape
        rows = group * hidden_width
        shapes += [
            jax.ShapeDtypeStruct((cells, slots, 128), jnp.float32),
            jax.ShapeDtypeStruct((cells, 128), jnp.int32),
            jax.ShapeDtypeStruct((layers, rows, group * basis_count), jnp.bfloat16),
            jax.ShapeDtypeStruct((layers, hidden_width, chunk), jnp.float32),
        ]
        scratch = [pltpu.VMEM(outer + extra[0].shape[3:], extra[0].dtype)]
        units += 1
    return pl.pallas_call(
        functools.partial(halo_kernel, bool(extra)),
        out_shape=shapes,
        in_specs=[vmem] * (1 + len(extra)),
        out_specs=[vmem] * len(shapes),
        scratch_shapes=scratch
        + [
            pltpu.SemaphoreType.DMA((2,)),
            pltpu.SemaphoreType.DMA((len(sides), 2, units)),
            pltpu.SemaphoreType.DMA((len(sides), 2, units)),
        ],
        compiler_params=pltpu.CompilerParams(collective_id=identity, has_side_effects=True),
        name="halo",
    )(state, *extra)


def total_kernel(axes, part, out, held, local_sem, send_sem, recv_sem):
    barrier = pltpu.get_barrier_semaphore()
    sizes = [lax.axis_size(axis) for axis in axes]
    places = [lax.axis_index(axis) for axis in axes]
    greeted = 0
    for axis, size, me in zip(axes, sizes, places):
        for step in range(1, size):
            pl.semaphore_signal(
                barrier, inc=1, device_id={axis: lax.rem(me + step, size)}, device_id_type=MESH
            )
            greeted += 1
    own = pltpu.make_async_copy(part, held.at[places[2], places[1], places[0]], local_sem)
    own.start()
    pl.semaphore_wait(barrier, greeted)
    own.wait()
    for stage, (axis, size, me) in enumerate(zip(axes, sizes, places)):
        if stage == 0:
            view = held.at[places[2], places[1], places[0]]
        elif stage == 1:
            view = held.at[places[2], places[1]]
        else:
            view = held.at[places[2]]
        copies = []
        for step in range(1, size):
            copy = pltpu.make_async_remote_copy(
                src_ref=view,
                dst_ref=view,
                send_sem=send_sem.at[stage, step],
                recv_sem=recv_sem.at[stage, step],
                device_id={axis: lax.rem(me + step, size)},
                device_id_type=MESH,
            )
            copy.start()
            copies.append(copy)
        for copy in copies:
            copy.wait()
    out[0] = jnp.sum(held[...]) / (part.shape[0] * part.shape[1])


def summed(part, axes, identity):
    sizes = [lax.axis_size(axis) for axis in axes]
    vmem = pl.BlockSpec(memory_space=pltpu.VMEM)
    return pl.pallas_call(
        functools.partial(total_kernel, axes),
        out_shape=jax.ShapeDtypeStruct((1,), part.dtype),
        in_specs=[vmem],
        out_specs=pl.BlockSpec(memory_space=pltpu.SMEM),
        scratch_shapes=[
            pltpu.VMEM((sizes[2], sizes[1], sizes[0]) + part.shape, part.dtype),
            pltpu.SemaphoreType.DMA,
            pltpu.SemaphoreType.DMA((3, max(sizes))),
            pltpu.SemaphoreType.DMA((3, max(sizes))),
        ],
        compiler_params=pltpu.CompilerParams(collective_id=identity, has_side_effects=True),
        name="total",
    )(part)


def layer_kernel(
    grid_dims,
    max_chunks,
    layer,
    counts,
    places,
    feats,
    radial_blocks,
    bias_wide,
    radial_out_all,
    atom_in_all,
    atom_bias_all,
    atom_out_all,
    readout_in,
    readout_out,
    out,
    part_out,
    fresh,
    spots,
    near_place,
    near_state,
    edges,
    plain_table,
    turned_table,
):
    deep, tall = grid_dims
    cell = pl.program_id(0)
    at_x = lax.div(cell, deep * tall)
    at_y = lax.rem(lax.div(cell, tall), deep)
    at_z = lax.rem(cell, tall)
    pad_y, pad_z = deep + 2, tall + 2
    slots = feats.shape[1]
    width = feats.shape[2] // 4
    radial_out = radial_out_all.at[layer]
    atom_out = atom_out_all.at[layer]
    hidden_width = radial_out.shape[0]
    basis_count = radial_blocks.shape[2] // group

    @pl.when(cell == 0)
    def _():
        part_out[...] = jnp.zeros(part_out.shape, part_out.dtype)

    lane = lax.broadcasted_iota(jnp.int32, (slots, width), 1)

    def cell_index(dx, dy, dz):
        return ((at_x + dx) * pad_y + at_y + dy) * pad_z + at_z + dz

    home = cell_index(1, 1, 1)
    total = 0
    own_start = 0
    for dx in range(3):
        for dy in range(3):
            for dz in range(3):
                index = cell_index(dx, dy, dz)
                if (dx, dy, dz) == (1, 1, 1):
                    own_start = total
                shift = jnp.where(
                    lane == 0, float(dx - 1), jnp.where(lane == 1, float(dy - 1), float(dz - 1))
                )
                near_place[pl.ds(total, slots), :] = places[index] + shift * cutoff
                block = feats[index].astype(jnp.float32)
                for part in range(4):
                    near_state[part, pl.ds(total, slots), :] = block[
                        :, part * width : (part + 1) * width
                    ]
                total = total + counts[index, 0]
    blank = jnp.zeros((chunk, width), jnp.float32)
    near_place[pl.ds(total, chunk), :] = blank
    for part in range(4):
        near_state[part, pl.ds(total, chunk), :] = blank
    chunks = lax.div(total + chunk - 1, chunk)

    @pl.loop(0, chunks)
    def _(step):
        rows = pl.ds(pl.multiple_of(step * chunk, chunk), chunk)
        near = near_place[rows, :].T[:8, :]
        mine = places[home]
        col = step * chunk + lax.broadcasted_iota(jnp.int32, (slots, chunk), 1)
        row = lax.broadcasted_iota(jnp.int32, (slots, chunk), 0)
        unused = jnp.logical_or(col == own_start + row, col >= total)
        offset = [near[k : k + 1, :] - mine[:, k : k + 1] for k in range(3)]
        square = offset[0] * offset[0] + offset[1] * offset[1] + offset[2] * offset[2]
        distance = jnp.sqrt(square + jnp.where(unused, 1.0, 0.0))
        inverse = 1.0 / distance
        smooth = 0.5 * (jnp.cos(math.pi / cutoff * distance) + 1.0)
        spots[0, :, rows] = distance
        spots[1, :, rows] = jnp.where(
            jnp.logical_and(distance < cutoff, jnp.logical_not(unused)), smooth, 0.0
        )
        for k in range(3):
            spots[k + 2, :, rows] = offset[k] * inverse
        half = jnp.dot(
            near_state[0, rows, :].astype(jnp.bfloat16),
            (0.5 * atom_in_all[layer].astype(jnp.float32)).astype(jnp.bfloat16),
            preferred_element_type=jnp.float32,
        ) + 0.5 * atom_bias_all[layer : layer + 1, :]
        hidden = (half + half * jnp.tanh(half)).astype(jnp.bfloat16)
        gates = jnp.dot(hidden, atom_out[...], preferred_element_type=jnp.float32).astype(
            jnp.bfloat16
        )
        plain_table[rows, :width] = gates[:, :width]
        gate_b = gates[:, width : 2 * width].astype(jnp.float32)
        gate_c = gates[:, 2 * width : 3 * width]
        gate_g = gates[:, 3 * width :].astype(jnp.float32)
        for part in range(3):
            vector = near_state[part + 1, rows, :]
            plain_table[rows, (part + 1) * width : (part + 2) * width] = (gate_b * vector).astype(
                jnp.bfloat16
            )
            turned_table[part, rows, :width] = gate_c
            turned_table[part, rows, width:] = (gate_g * vector).astype(jnp.bfloat16)

    own_count = counts[home, 0]
    fresh[...] = jnp.zeros(fresh.shape, fresh.dtype)
    sharpness = 0.5 * ((basis_count - 1) / cutoff) ** 2

    @pl.loop(0, lax.div(own_count + group - 1, group))
    def _(turn):
        first = pl.multiple_of(turn * group, group)

        def form_edges(step):
            columns = slice(step * chunk, (step + 1) * chunk)
            receivers = pl.ds(first, group)
            distance = spots[0, receivers, columns]
            centers = lax.broadcasted_iota(jnp.int32, (1, basis_count, chunk), 1).astype(
                jnp.float32
            ) * (cutoff / (basis_count - 1))
            gap = distance[:, None, :] - centers
            basis = jnp.exp(-sharpness * gap * gap).reshape(group * basis_count, chunk)
            half = jnp.dot(
                radial_blocks[layer],
                basis.astype(jnp.bfloat16),
                preferred_element_type=jnp.float32,
            ).reshape(group, hidden_width, chunk) + bias_wide[layer][None]
            active = (half + half * jnp.tanh(half)) * spots[1, receivers, columns][:, None, :]
            edges[0, :, columns] = active.reshape(group * hidden_width, chunk).astype(jnp.bfloat16)
            for k in range(3):
                unit = spots[k + 2, receivers, columns][:, None, :]
                edges[k + 1, :, columns] = (
                    (active * unit).reshape(group * hidden_width, chunk).astype(jnp.bfloat16)
                )

        for used in range(1, max_chunks + 1):

            @pl.when(chunks == used)
            def _(used=used):
                span = used * chunk
                for step in range(used):
                    form_edges(step)

                def contracted(left, right, filters):
                    product = jnp.dot(left, right, preferred_element_type=jnp.float32)
                    product = product.reshape(group, hidden_width, 2 * width)
                    return (
                        jnp.sum(product[:, :, :width] * filters[0], axis=1),
                        jnp.sum(product[:, :, width:] * filters[1], axis=1),
                    )

                bank = [
                    radial_out[:, part * width : (part + 1) * width].astype(jnp.float32)[None]
                    for part in range(4)
                ]
                flat = edges[0, :, :span]
                scalar, vector0 = contracted(flat, plain_table[:span, : 2 * width], (bank[0], bank[1]))
                vector1, vector2 = contracted(flat, plain_table[:span, 2 * width :], (bank[1], bank[1]))
                vectors = [vector0, vector1, vector2]
                for k in range(3):
                    along, project = contracted(
                        edges[k + 1, :, :span], turned_table[k, :span, :], (bank[2], bank[3])
                    )
                    vectors[k] = vectors[k] + along
                    scalar = scalar + project
                receivers = first + lax.broadcasted_iota(jnp.int32, (group, width), 0)
                alive = receivers < own_count
                for part, change in enumerate([scalar] + vectors):
                    before = near_state[part, pl.ds(own_start + first, group), :]
                    after = jnp.where(alive, before + message_scale * change, 0.0)
                    fresh[pl.ds(first, group), part * width : (part + 1) * width] = after

    rounded = fresh[...].astype(jnp.bfloat16)
    out[0] = rounded
    if layer == radial_out_all.shape[0] - 1:
        read = lax.dot_general(
            rounded[:, :width],
            readout_in[...],
            (((1,), (1,)), ((), ())),
            preferred_element_type=jnp.float32,
        )
        read = read / (1.0 + jnp.exp(-read)) * readout_out[...]
        alive = lax.broadcasted_iota(jnp.int32, read.shape, 0) < own_count
        amount = jnp.sum(jnp.where(alive, read, 0.0), axis=(0, 1), keepdims=True)
        part_out[...] += jnp.broadcast_to(amount, part_out.shape)


def layer_update(layer, cells_shape, counts, places, feats, params):
    cells_wide, cells_deep, cells_tall = cells_shape
    total_cells = cells_wide * cells_deep * cells_tall
    slots = feats.shape[1]
    width = feats.shape[2] // 4
    hidden_width = params[1].shape[1]
    max_chunks = -(-27 * slots // chunk)
    span = max_chunks * chunk
    store = 27 * slots + chunk + slots
    store = -(-store // 8) * 8
    vmem = pl.BlockSpec(memory_space=pltpu.VMEM)
    return pl.pallas_call(
        functools.partial(layer_kernel, (cells_deep, cells_tall), max_chunks, layer),
        grid=(total_cells,),
        out_shape=(
            jax.ShapeDtypeStruct((total_cells, slots, 4 * width), jnp.bfloat16),
            jax.ShapeDtypeStruct((8, 128), jnp.float32),
        ),
        in_specs=[pl.BlockSpec(memory_space=pltpu.SMEM)] + [vmem] * (2 + len(params)),
        out_specs=(
            pl.BlockSpec((1, slots, 4 * width), lambda i: (i, 0, 0)),
            pl.BlockSpec((8, 128), lambda i: (0, 0)),
        ),
        scratch_shapes=[
            pltpu.VMEM((slots, 4 * width), jnp.float32),
            pltpu.VMEM((5, slots, span), jnp.float32),
            pltpu.VMEM((store, width), jnp.float32),
            pltpu.VMEM((4, store, width), jnp.float32),
            pltpu.VMEM((4, group * hidden_width, span), jnp.bfloat16),
            pltpu.VMEM((span, 4 * width), jnp.bfloat16),
            pltpu.VMEM((3, span, 2 * width), jnp.bfloat16),
        ],
        compiler_params=pltpu.CompilerParams(vmem_limit_bytes=56 << 20),
        name="message_layer",
    )(counts, places, feats, *params)


def on_device(
    positions,
    counts,
    scalars,
    vectors,
    radial_in,
    radial_bias,
    radial_out,
    atom_in,
    atom_bias,
    atom_out,
    readout_in,
    readout_out,
):
    cells_wide, cells_deep, cells_tall, slots, width = scalars.shape
    cells_shape = (cells_wide, cells_deep, cells_tall)
    level = jnp.broadcast_to(counts.astype(jnp.float32)[..., None, None], cells_shape + (1, slots))
    geometry = jnp.concatenate([positions, level], axis=3)
    geometry = jnp.pad(geometry, ((0, 0),) * 3 + ((0, 8 - geometry.shape[3]), (0, 128 - slots)))
    state = jnp.concatenate(
        [scalars, vectors.reshape(cells_shape + (slots, 3 * width))], axis=-1
    )
    params = (radial_out, atom_in, atom_bias, atom_out, readout_in.T, readout_out[None, :])
    for layer in range(radial_in.shape[0]):
        if layer == 0:
            feats, places, near_counts, blocks, bias_wide = extended(
                state, 0, (geometry, radial_in, radial_bias)
            )
            params = (blocks, bias_wide) + params
        else:
            (feats,) = extended(state, layer)
        state, part = layer_update(
            layer, cells_shape, near_counts, places, feats.reshape(-1, slots, 4 * width), params
        )
        state = state.reshape(cells_shape + (slots, 4 * width))
    scalar_state = state[..., :width]
    vector_state = state[..., width:].reshape(cells_shape + (slots, 3, width))
    energy = summed(part, ("gz", "gx", "gy"), radial_in.shape[0])
    return (scalar_state, vector_state, energy)


def solution(mesh):
    block = P("gx", "gy", "gz")
    in_specs = (block,) * 4 + (P(),) * 8
    out_specs = (block, block, P())
    return jax.shard_map(
        on_device, mesh=mesh, in_specs=in_specs, out_specs=out_specs, check_vma=False
    )
```

```python
import functools
import math

import jax
import jax.numpy as jnp
from jax import lax
from jax.experimental import pallas as pl
from jax.experimental.pallas import tpu as pltpu
from jax.sharding import PartitionSpec as P

cutoff = 5.0
message_scale = 0.5
group = 8
chunk = 256


MESH = pl.DeviceIdType.MESH
sides = (("gy", 1), ("gx", 0), ("gz", 2))
other_sides = (("gy", 1), ("gz", 2), ("gx", 0))


def ring(axis):
    me = lax.axis_index(axis)
    count = lax.axis_size(axis)
    return lax.rem(me + 1, count), lax.rem(me + count - 1, count)


def prepare(ground, radial_in, radial_bias, places, counts, radial_block, bias_wide):
    wide, deep, tall = ground.shape[:3]
    slots = places.shape[1]
    layers, basis_count, hidden_width = radial_in.shape
    for x in range(wide):
        for y in range(deep):
            for z in range(tall):
                index = (x * deep + y) * tall + z
                tile = ground[x, y, z, 0]
                places[index, :, :8] = tile.T[:slots, :]
                counts[index : index + 1, :] = tile[3:4, :].astype(jnp.int32)
    box = (group, hidden_width, group * basis_count)
    owner = lax.div(lax.broadcasted_iota(jnp.int32, box, 2), basis_count)
    match = owner == lax.broadcasted_iota(jnp.int32, box, 0)
    for layer in range(layers):
        small = 0.5 * radial_in[layer].astype(jnp.float32)
        tall_form = jnp.concatenate([small] * group, axis=0)
        wide_form = jnp.concatenate([tall_form] * (128 // hidden_width), axis=1).T[:hidden_width]
        spread = jnp.where(match, jnp.broadcast_to(wide_form[None], box), 0.0)
        radial_block[layer] = spread.reshape(radial_block.shape[1:]).astype(jnp.bfloat16)
        bias = 0.5 * radial_bias[layer : layer + 1, :]
        bias = jnp.concatenate([bias] * (128 // hidden_width), axis=1)
        bias_wide[layer] = jnp.broadcast_to(bias, (chunk, 128)).T[:hidden_width]


def halo_kernel(first, *refs):
    if first:
        blocks, (radial_in, radial_bias) = refs[:3], refs[3:5]
        made = refs[7:11]
        ground, local_sem, send_sem, recv_sem = refs[11:]
        pads = refs[5:7] + (ground,)
    else:
        blocks, pads = refs[:2], refs[2:4]
        local_sem, send_sem, recv_sem = refs[4:]
    dims = blocks[0].shape[:3]
    around = {axis: ring(axis) for axis, _ in sides}
    barrier = pltpu.get_barrier_semaphore()
    for axis, _ in sides:
        for side in around[axis]:
            pl.semaphore_signal(barrier, inc=1, device_id={axis: side}, device_id_type=MESH)
    units = []
    for block, pad in zip(blocks, pads):
        for part in range(block.shape[3]):
            units.append((block, pad, pl.ds(part, 1), sides))
    units = units[::-1]
    units[-1] = units[-1][:3] + (other_sides,)
    center = tuple(pl.ds(1, extent) for extent in dims)
    own = []
    for place, (block, pad) in enumerate(zip(blocks, pads)):
        own.append(pltpu.make_async_copy(block, pad.at[center], local_sem.at[place]))
        own[-1].start()
    pl.semaphore_wait(barrier, 2 * len(sides))
    sent = {}

    def send(stage, number):
        block, pad, part, order = units[number]
        axis, dim = order[stage]
        done = [d for _, d in order[:stage]]
        extent = dims[dim]
        for way, (source, target) in enumerate(((extent, 0), (1, extent + 1))):
            region = [
                pl.ds(0, dims[d] + 2) if d in done else pl.ds(1, dims[d]) for d in range(3)
            ]
            region[dim] = pl.ds(target, 1)
            to = pad.at[tuple(region) + (part,)]
            if stage == 0:
                region = [pl.ds(0, dims[d]) for d in range(3)]
                region[dim] = pl.ds(source - 1, 1)
                come = block.at[tuple(region) + (part,)]
            else:
                region[dim] = pl.ds(source, 1)
                come = pad.at[tuple(region) + (part,)]
            copy = pltpu.make_async_remote_copy(
                src_ref=come,
                dst_ref=to,
                send_sem=send_sem.at[stage, way, number],
                recv_sem=recv_sem.at[stage, way, number],
                device_id={axis: around[axis][way]},
                device_id_type=MESH,
            )
            copy.start()
            sent[stage, way, number] = copy

    for number in range(len(units)):
        send(0, number)
    for copy in own:
        copy.wait()
    for stage in range(1, len(sides) + 1):
        for number in range(len(units)):
            for way in range(2):
                sent[stage - 1, way, number].wait_recv()
            if stage < len(sides):
                send(stage, number)
            elif number == 0 and first:
                prepare(ground, radial_in, radial_bias, *made)
    for copy in sent.values():
        copy.wait_send()


def extended(states, identity, extra=()):
    dims = states[0].shape[:3]
    slots = states[0].shape[4]
    vmem = pl.BlockSpec(memory_space=pltpu.VMEM)
    outer = tuple(d + 2 for d in dims)
    cells = math.prod(outer)
    shapes = [jax.ShapeDtypeStruct(outer + state.shape[3:], state.dtype) for state in states]
    scratch = []
    units = sum(state.shape[3] for state in states)
    if extra:
        layers, basis_count, hidden_width = extra[1].shape
        rows = group * hidden_width
        shapes += [
            jax.ShapeDtypeStruct((cells, slots, 128), jnp.float32),
            jax.ShapeDtypeStruct((cells, 128), jnp.int32),
            jax.ShapeDtypeStruct((layers, rows, group * basis_count), jnp.bfloat16),
            jax.ShapeDtypeStruct((layers, hidden_width, chunk), jnp.float32),
        ]
        scratch = [pltpu.VMEM(outer + extra[0].shape[3:], extra[0].dtype)]
        units += 1
    return pl.pallas_call(
        functools.partial(halo_kernel, bool(extra)),
        out_shape=shapes,
        in_specs=[vmem] * (len(states) + len(extra)),
        out_specs=[vmem] * len(shapes),
        scratch_shapes=scratch
        + [
            pltpu.SemaphoreType.DMA((3,)),
            pltpu.SemaphoreType.DMA((len(sides), 2, units)),
            pltpu.SemaphoreType.DMA((len(sides), 2, units)),
        ],
        compiler_params=pltpu.CompilerParams(collective_id=identity, has_side_effects=True),
        name="halo",
    )(*states, *extra)


def total_kernel(axes, part, out, held, local_sem, send_sem, recv_sem):
    barrier = pltpu.get_barrier_semaphore()
    sizes = [lax.axis_size(axis) for axis in axes]
    places = [lax.axis_index(axis) for axis in axes]
    greeted = 0
    for axis, size, me in zip(axes, sizes, places):
        for step in range(1, size):
            pl.semaphore_signal(
                barrier, inc=1, device_id={axis: lax.rem(me + step, size)}, device_id_type=MESH
            )
            greeted += 1
    own = pltpu.make_async_copy(part, held.at[places[2], places[1], places[0]], local_sem)
    own.start()
    pl.semaphore_wait(barrier, greeted)
    own.wait()
    for stage, (axis, size, me) in enumerate(zip(axes, sizes, places)):
        if stage == 0:
            view = held.at[places[2], places[1], places[0]]
        elif stage == 1:
            view = held.at[places[2], places[1]]
        else:
            view = held.at[places[2]]
        copies = []
        for step in range(1, size):
            copy = pltpu.make_async_remote_copy(
                src_ref=view,
                dst_ref=view,
                send_sem=send_sem.at[stage, step],
                recv_sem=recv_sem.at[stage, step],
                device_id={axis: lax.rem(me + step, size)},
                device_id_type=MESH,
            )
            copy.start()
            copies.append(copy)
        for copy in copies:
            copy.wait()
    out[0] = jnp.sum(held[...]) / (part.shape[0] * part.shape[1])


def summed(part, axes, identity):
    sizes = [lax.axis_size(axis) for axis in axes]
    vmem = pl.BlockSpec(memory_space=pltpu.VMEM)
    return pl.pallas_call(
        functools.partial(total_kernel, axes),
        out_shape=jax.ShapeDtypeStruct((1,), part.dtype),
        in_specs=[vmem],
        out_specs=pl.BlockSpec(memory_space=pltpu.SMEM),
        scratch_shapes=[
            pltpu.VMEM((sizes[2], sizes[1], sizes[0]) + part.shape, part.dtype),
            pltpu.SemaphoreType.DMA,
            pltpu.SemaphoreType.DMA((3, max(sizes))),
            pltpu.SemaphoreType.DMA((3, max(sizes))),
        ],
        compiler_params=pltpu.CompilerParams(collective_id=identity, has_side_effects=True),
        name="total",
    )(part)


def layer_kernel(
    grid_dims,
    max_chunks,
    layer,
    counts,
    places,
    near_scalars,
    near_vectors,
    radial_blocks,
    bias_wide,
    radial_out_all,
    atom_in_all,
    atom_bias_all,
    atom_out_all,
    readout_in,
    readout_out,
    scalars_out,
    vectors_out,
    part_out,
    fresh,
    spots,
    near_place,
    near_state,
    edges,
    plain_table,
    turned_table,
):
    deep, tall = grid_dims
    cell = pl.program_id(0)
    at_x = lax.div(cell, deep * tall)
    at_y = lax.rem(lax.div(cell, tall), deep)
    at_z = lax.rem(cell, tall)
    pad_y, pad_z = deep + 2, tall + 2
    slots, width = near_scalars.shape[2:]
    radial_out = radial_out_all.at[layer]
    atom_out = atom_out_all.at[layer]
    hidden_width = radial_out.shape[0]
    basis_count = radial_blocks.shape[2] // group

    @pl.when(cell == 0)
    def _():
        part_out[...] = jnp.zeros(part_out.shape, part_out.dtype)

    lane = lax.broadcasted_iota(jnp.int32, (slots, width), 1)

    def cell_index(dx, dy, dz):
        return ((at_x + dx) * pad_y + at_y + dy) * pad_z + at_z + dz

    home = cell_index(1, 1, 1)
    total = 0
    own_start = 0
    for dx in range(3):
        for dy in range(3):
            for dz in range(3):
                index = cell_index(dx, dy, dz)
                if (dx, dy, dz) == (1, 1, 1):
                    own_start = total
                shift = jnp.where(
                    lane == 0, float(dx - 1), jnp.where(lane == 1, float(dy - 1), float(dz - 1))
                )
                near_place[pl.ds(total, slots), :] = places[index] + shift * cutoff
                near_state[0, pl.ds(total, slots), :] = near_scalars[index, 0].astype(jnp.float32)
                for part in range(3):
                    near_state[part + 1, pl.ds(total, slots), :] = near_vectors[
                        index, part
                    ].astype(jnp.float32)
                total = total + counts[index, 0]
    blank = jnp.zeros((chunk, width), jnp.float32)
    near_place[pl.ds(total, chunk), :] = blank
    for part in range(4):
        near_state[part, pl.ds(total, chunk), :] = blank
    chunks = lax.div(total + chunk - 1, chunk)

    @pl.loop(0, chunks)
    def _(step):
        rows = pl.ds(pl.multiple_of(step * chunk, chunk), chunk)
        near = near_place[rows, :].T[:8, :]
        mine = places[home]
        col = step * chunk + lax.broadcasted_iota(jnp.int32, (slots, chunk), 1)
        row = lax.broadcasted_iota(jnp.int32, (slots, chunk), 0)
        unused = jnp.logical_or(col == own_start + row, col >= total)
        offset = [near[k : k + 1, :] - mine[:, k : k + 1] for k in range(3)]
        square = offset[0] * offset[0] + offset[1] * offset[1] + offset[2] * offset[2]
        distance = jnp.sqrt(square + jnp.where(unused, 1.0, 0.0))
        inverse = 1.0 / distance
        smooth = 0.5 * (jnp.cos(math.pi / cutoff * distance) + 1.0)
        spots[0, :, rows] = distance
        spots[1, :, rows] = jnp.where(
            jnp.logical_and(distance < cutoff, jnp.logical_not(unused)), smooth, 0.0
        )
        for k in range(3):
            spots[k + 2, :, rows] = offset[k] * inverse
        half = jnp.dot(
            near_state[0, rows, :].astype(jnp.bfloat16),
            (0.5 * atom_in_all[layer].astype(jnp.float32)).astype(jnp.bfloat16),
            preferred_element_type=jnp.float32,
        ) + 0.5 * atom_bias_all[layer : layer + 1, :]
        hidden = (half + half * jnp.tanh(half)).astype(jnp.bfloat16)
        gates = jnp.dot(hidden, atom_out[...], preferred_element_type=jnp.float32).astype(
            jnp.bfloat16
        )
        plain_table[rows, :width] = gates[:, :width]
        gate_b = gates[:, width : 2 * width].astype(jnp.float32)
        gate_c = gates[:, 2 * width : 3 * width]
        gate_g = gates[:, 3 * width :].astype(jnp.float32)
        for part in range(3):
            vector = near_state[part + 1, rows, :]
            plain_table[rows, (part + 1) * width : (part + 2) * width] = (gate_b * vector).astype(
                jnp.bfloat16
            )
            turned_table[part, rows, :width] = gate_c
            turned_table[part, rows, width:] = (gate_g * vector).astype(jnp.bfloat16)

    own_count = counts[home, 0]
    fresh[...] = jnp.zeros(fresh.shape, fresh.dtype)
    sharpness = 0.5 * ((basis_count - 1) / cutoff) ** 2

    @pl.loop(0, lax.div(own_count + group - 1, group))
    def _(turn):
        first = pl.multiple_of(turn * group, group)

        def form_edges(step):
            columns = slice(step * chunk, (step + 1) * chunk)
            receivers = pl.ds(first, group)
            distance = spots[0, receivers, columns]
            centers = lax.broadcasted_iota(jnp.int32, (1, basis_count, chunk), 1).astype(
                jnp.float32
            ) * (cutoff / (basis_count - 1))
            gap = distance[:, None, :] - centers
            basis = jnp.exp(-sharpness * gap * gap).reshape(group * basis_count, chunk)
            half = jnp.dot(
                radial_blocks[layer],
                basis.astype(jnp.bfloat16),
                preferred_element_type=jnp.float32,
            ).reshape(group, hidden_width, chunk) + bias_wide[layer][None]
            active = (half + half * jnp.tanh(half)) * spots[1, receivers, columns][:, None, :]
            edges[0, :, columns] = active.reshape(group * hidden_width, chunk).astype(jnp.bfloat16)
            for k in range(3):
                unit = spots[k + 2, receivers, columns][:, None, :]
                edges[k + 1, :, columns] = (
                    (active * unit).reshape(group * hidden_width, chunk).astype(jnp.bfloat16)
                )

        for used in range(1, max_chunks + 1):

            @pl.when(chunks == used)
            def _(used=used):
                span = used * chunk
                for step in range(used):
                    form_edges(step)

                def contracted(left, right, filters):
                    product = jnp.dot(left, right, preferred_element_type=jnp.float32)
                    product = product.reshape(group, hidden_width, 2 * width)
                    return (
                        jnp.sum(product[:, :, :width] * filters[0], axis=1),
                        jnp.sum(product[:, :, width:] * filters[1], axis=1),
                    )

                bank = [
                    radial_out[:, part * width : (part + 1) * width].astype(jnp.float32)[None]
                    for part in range(4)
                ]
                flat = edges[0, :, :span]
                scalar, vector0 = contracted(flat, plain_table[:span, : 2 * width], (bank[0], bank[1]))
                vector1, vector2 = contracted(flat, plain_table[:span, 2 * width :], (bank[1], bank[1]))
                vectors = [vector0, vector1, vector2]
                for k in range(3):
                    along, project = contracted(
                        edges[k + 1, :, :span], turned_table[k, :span, :], (bank[2], bank[3])
                    )
                    vectors[k] = vectors[k] + along
                    scalar = scalar + project
                receivers = first + lax.broadcasted_iota(jnp.int32, (group, width), 0)
                alive = receivers < own_count
                for part, change in enumerate([scalar] + vectors):
                    before = near_state[part, pl.ds(own_start + first, group), :]
                    after = jnp.where(alive, before + message_scale * change, 0.0)
                    fresh[pl.ds(first, group), part * width : (part + 1) * width] = after

    rounded = fresh[...].astype(jnp.bfloat16)
    scalars_out[0, 0] = rounded[:, :width]
    for part in range(3):
        vectors_out[0, part] = rounded[:, (part + 1) * width : (part + 2) * width]
    if layer == radial_out_all.shape[0] - 1:
        read = lax.dot_general(
            rounded[:, :width],
            readout_in[...],
            (((1,), (1,)), ((), ())),
            preferred_element_type=jnp.float32,
        )
        read = read / (1.0 + jnp.exp(-read)) * readout_out[...]
        alive = lax.broadcasted_iota(jnp.int32, read.shape, 0) < own_count
        amount = jnp.sum(jnp.where(alive, read, 0.0), axis=(0, 1), keepdims=True)
        part_out[...] += jnp.broadcast_to(amount, part_out.shape)


def layer_update(layer, cells_shape, counts, places, states, params):
    cells_wide, cells_deep, cells_tall = cells_shape
    total_cells = cells_wide * cells_deep * cells_tall
    states = [state.reshape((-1,) + state.shape[3:]) for state in states]
    slots, width = states[0].shape[2:]
    hidden_width = params[1].shape[1]
    max_chunks = -(-27 * slots // chunk)
    span = max_chunks * chunk
    store = 27 * slots + chunk + slots
    store = -(-store // 8) * 8
    vmem = pl.BlockSpec(memory_space=pltpu.VMEM)
    return pl.pallas_call(
        functools.partial(layer_kernel, (cells_deep, cells_tall), max_chunks, layer),
        grid=(total_cells,),
        out_shape=(
            jax.ShapeDtypeStruct((total_cells, 1, slots, width), jnp.bfloat16),
            jax.ShapeDtypeStruct((total_cells, 3, slots, width), jnp.bfloat16),
            jax.ShapeDtypeStruct((8, 128), jnp.float32),
        ),
        in_specs=[pl.BlockSpec(memory_space=pltpu.SMEM)] + [vmem] * (3 + len(params)),
        out_specs=(
            pl.BlockSpec((1, 1, slots, width), lambda i: (i, 0, 0, 0)),
            pl.BlockSpec((1, 3, slots, width), lambda i: (i, 0, 0, 0)),
            pl.BlockSpec((8, 128), lambda i: (0, 0)),
        ),
        scratch_shapes=[
            pltpu.VMEM((slots, 4 * width), jnp.float32),
            pltpu.VMEM((5, slots, span), jnp.float32),
            pltpu.VMEM((store, width), jnp.float32),
            pltpu.VMEM((4, store, width), jnp.float32),
            pltpu.VMEM((4, group * hidden_width, span), jnp.bfloat16),
            pltpu.VMEM((span, 4 * width), jnp.bfloat16),
            pltpu.VMEM((3, span, 2 * width), jnp.bfloat16),
        ],
        compiler_params=pltpu.CompilerParams(vmem_limit_bytes=56 << 20),
        name="message_layer",
    )(counts, places, *states, *params)


def on_device(
    positions,
    counts,
    scalars,
    vectors,
    radial_in,
    radial_bias,
    radial_out,
    atom_in,
    atom_bias,
    atom_out,
    readout_in,
    readout_out,
):
    cells_wide, cells_deep, cells_tall, slots, width = scalars.shape
    cells_shape = (cells_wide, cells_deep, cells_tall)
    level = jnp.broadcast_to(counts.astype(jnp.float32)[..., None, None], cells_shape + (1, slots))
    geometry = jnp.concatenate([positions, level], axis=3)
    geometry = jnp.pad(geometry, ((0, 0),) * 3 + ((0, 8 - geometry.shape[3]), (0, 128 - slots)))
    geometry = geometry[:, :, :, None]
    states = [scalars[:, :, :, None], vectors.transpose(0, 1, 2, 4, 3, 5)]
    params = (radial_out, atom_in, atom_bias, atom_out, readout_in.T, readout_out[None, :])
    for layer in range(radial_in.shape[0]):
        if layer == 0:
            *states, places, near_counts, blocks, bias_wide = extended(
                states, 0, (geometry, radial_in, radial_bias)
            )
            params = (blocks, bias_wide) + params
        else:
            states = extended(states, layer)
        *states, part = layer_update(layer, cells_shape, near_counts, places, states, params)
        states = [state.reshape(cells_shape + state.shape[1:]) for state in states]
    scalar_state = states[0][:, :, :, 0]
    vector_state = states[1].transpose(0, 1, 2, 4, 3, 5)
    energy = summed(part, ("gz", "gx", "gy"), radial_in.shape[0])
    return (scalar_state, vector_state, energy)


def solution(mesh):
    block = P("gx", "gy", "gz")
    in_specs = (block,) * 4 + (P(),) * 8
    out_specs = (block, block, P())
    return jax.shard_map(
        on_device, mesh=mesh, in_specs=in_specs, out_specs=out_specs, check_vma=False
    )
```
